32 devices in a mesh: chan: 2 (over x), stn: 16 (over z, y, core).
Axes of the slice: x: 2, y: 2, z: 4, core: 2. Of those that a mesh axis runs over, the one named last changes fastest.
Arguments:
- volts: bfloat16 [2, 128, 38, 3072], P(None, 'stn', 'chan'), may hold values from -6 to 6
- fir: float32 [16, 3072], replicated, may hold values from -0.02734375 to 0.02734375
- gains: float32 [2, 24, 128, 128], P(None, 'chan', 'stn'), may hold values from -4 to 4
- delays: float32 [288, 128], replicated, may hold values from -16 to 16
- subsets: int32 [288, 128], replicated, may hold values from 0 to 127, as said below
- beam_sizes: int32 [288], replicated, may hold values from 1 to 128
- station_ids: int32 [128], replicated, may hold values from 0 to 127, each once
- beam_order: int32 [288], replicated, may hold values from 0 to 287, each once
Outputs:
- beams: bfloat16 [2, 24, 128, 288, 8], P(None, 'chan', None, 'stn')
The draws below stay inside these ranges and needn't reach their ends.
Inputs may be any that keep to these rules, and one draw needn't show every extreme that they name: Each row of subsets lists every station id once; beam b uses its first beam_sizes[b] entries.
All inputs are finite; a program needn't handle non-finite values.
Results may differ from the reference program's by a relative error of at most 0.0057.
Values may be sent and summed in bfloat16 or wider, within the bound.
A program may use at most 64 MiB of HBM per device.

```python
import math
import jax
import jax.numpy as jnp
from jax import lax

FR_DEV = 4
TAPS = 16
RADIX = 24
SUBLEN = 128
BEAMS = 288
NCH = 3072
STN = 128
BLOCK = 19
FRAMES = 8
N_CHAN = 2


def draw_subsets(key, part):
    beam_keys = jax.random.split(key, BEAMS)
    return jax.vmap(lambda subkey: jax.random.permutation(subkey, STN))(beam_keys).astype(jnp.int32)


def place_ends(values, own_key, low, largest):
    spot = [jax.random.randint(jax.random.fold_in(own_key, axis), (), 0, length) for axis, length in enumerate(values.shape)]
    longest = values.shape.index(max(values.shape))
    beside = spot[:longest] + [(spot[longest] + 1) % values.shape[longest]] + spot[longest + 1:]
    return values.at[tuple(spot)].set(low).at[tuple(beside)].set(largest)


def steps_of(stream_key, shape, shards, least, largest):
    gain, own = 1.0, jax.random.fold_in(stream_key, 6)
    for position, shards_of in shards:
        draws = jnp.exp(jax.random.uniform(jax.random.fold_in(own, position), (shards_of,), jnp.float32, least / len(shards), largest / len(shards)))
        gain = gain * jnp.repeat(draws, shape[position] // shards_of).reshape([-1 if axis == position else 1 for axis in range(len(shape))])
    return gain


def scatter_about(stream_key, dims, spread, reach, shards=(), dtype=jnp.bfloat16):
    level = steps_of(stream_key, dims, shards, -0.22, 0.18) if shards else 1.0
    drawn = jax.random.normal(stream_key, dims, jnp.float32) * spread * level
    return jnp.minimum(jnp.maximum(drawn, -reach), reach).astype(dtype)


def setup_inputs(seed: int = 0) -> dict:
    seeds = jax.random.split(jax.random.key(seed), 9)
    volts = scatter_about(seeds[0], (2, STN, N_CHAN * BLOCK, NCH), 1.0, 6.0, ((1, 16), (2, 2)))
    fir = scatter_about(seeds[1], (TAPS, NCH), (TAPS * NCH) ** -0.5, 0.02734375, (), jnp.float32)
    gains = scatter_about(seeds[2], (2, RADIX, SUBLEN, STN), 0.7, 4.0, ((1, 2), (2, 16)), jnp.float32)
    delays = jnp.clip(jax.random.uniform(seeds[3], (BEAMS, STN), jnp.float32, -16.0, 16.0), -16.0, 16.0)
    subsets = draw_subsets(jax.random.fold_in(seeds[8], 71), 0)
    beam_sizes = place_ends(jax.random.randint(seeds[5], (BEAMS,), 1, STN + 1), jax.random.fold_in(seeds[5], 1), 1, STN).astype(jnp.int32)
    station_ids = jax.random.permutation(seeds[6], STN).astype(jnp.int32)
    beam_order = jax.random.permutation(seeds[7], BEAMS).astype(jnp.int32)
    return dict(volts=volts, fir=fir, gains=gains, delays=delays, subsets=subsets, beam_sizes=beam_sizes, station_ids=station_ids, beam_order=beam_order)


full_turn = 2.0 * math.pi

def membership(subsets, beam_sizes):
    beam_count = subsets.shape[0]
    station_count = subsets.shape[1]
    beam_rows = jnp.broadcast_to(jnp.arange(beam_count)[:, None], (beam_count, station_count))
    valid = (jnp.arange(station_count)[None, :] < beam_sizes[:, None]).astype(jnp.float32)
    return jnp.zeros((beam_count, station_count), jnp.float32).at[beam_rows, subsets].max(valid)

def channelize(block, fir):

    def add_tap(tap_index, total):
        piece = lax.dynamic_slice_in_dim(block, tap_index, FR_DEV, 2).astype(jnp.float32)
        coefs = lax.dynamic_index_in_dim(fir, tap_index, 0, keepdims=False)
        return total + coefs * piece
    filtered = lax.fori_loop(0, TAPS, add_tap, jnp.zeros((2, STN, FR_DEV, NCH), jnp.float32))
    spectrum = jnp.fft.fft(lax.complex(filtered[0], filtered[1]), axis=-1)
    paired = jnp.stack([jnp.real(spectrum), jnp.imag(spectrum)]).astype(jnp.bfloat16)
    return paired.reshape(2, STN, FR_DEV, SUBLEN, RADIX)

def reference(volts, fir, gains, delays, subsets, beam_sizes, station_ids, beam_order):
    blocks = volts.reshape(2, STN, N_CHAN, BLOCK, NCH).transpose(2, 0, 1, 3, 4)
    spectra = lax.map(lambda block: channelize(block, fir), blocks)
    per_radix = spectra.transpose(5, 1, 4, 0, 3, 2).reshape(RADIX, 2, SUBLEN, FRAMES, STN)
    member = membership(subsets, beam_sizes)
    weight_mask = member[:, station_ids][beam_order] * lax.rsqrt(beam_sizes[beam_order].astype(jnp.float32))[:, None]
    delay_rows = delays[:, station_ids][beam_order]
    gain_rows = jnp.take(gains, station_ids, axis=3)

    def form_beams(inputs):
        radix_index, spectra_part = inputs
        gain_part = lax.dynamic_index_in_dim(gain_rows, radix_index, 1, keepdims=False)
        chan_index = (RADIX * jnp.arange(SUBLEN) + radix_index).astype(jnp.float32)
        angle = (full_turn * chan_index)[:, None, None] * delay_rows[None] / NCH
        cosine = jnp.cos(angle)
        sine = jnp.sin(angle)
        gain_real = gain_part[0][:, None, :]
        gain_imag = gain_part[1][:, None, :]
        weight_real = ((gain_real * cosine + gain_imag * sine) * weight_mask[None]).astype(jnp.bfloat16).astype(jnp.float32)
        weight_imag = ((gain_imag * cosine - gain_real * sine) * weight_mask[None]).astype(jnp.bfloat16).astype(jnp.float32)
        data_real = spectra_part[0].astype(jnp.float32)
        data_imag = spectra_part[1].astype(jnp.float32)
        beam_real = jnp.einsum('cbr,ctr->cbt', weight_real, data_real) - jnp.einsum('cbr,ctr->cbt', weight_imag, data_imag)
        beam_imag = jnp.einsum('cbr,ctr->cbt', weight_real, data_imag) + jnp.einsum('cbr,ctr->cbt', weight_imag, data_real)
        return jnp.stack([beam_real, beam_imag]).astype(jnp.bfloat16)
    formed = lax.map(form_beams, (jnp.arange(RADIX), per_radix))
    return formed.transpose(1, 0, 2, 3, 4)
```

```python
import functools
import math

import jax
import jax.numpy as jnp
import numpy as np
from jax import lax
from jax.experimental import pallas as pl
from jax.experimental.pallas import tpu as pltpu
from jax.sharding import PartitionSpec as P

RADIX = 24
SUBLEN = 128
NCH = 3072


full_turn = 2.0 * math.pi


def membership(subsets, beam_sizes):
    beam_count = subsets.shape[0]
    station_count = subsets.shape[1]
    block_count = 8
    per_block = beam_count // block_count
    station_range = jnp.arange(station_count, dtype=jnp.int32)

    def one_block(inputs):
        rows, sizes = inputs
        valid = station_range[None, :] < sizes[:, None]
        listed = rows[:, :, None] == station_range[None, None, :]
        return jnp.any(listed & valid[:, :, None], axis=1).astype(jnp.float32)

    blocked = lax.map(
        one_block,
        (
            subsets.reshape(block_count, per_block, station_count),
            beam_sizes.reshape(block_count, per_block),
        ),
    )
    return blocked.reshape(beam_count, station_count)


def dft_table(length, modulus):
    index = jnp.arange(length)
    angle = (
        full_turn
        * (index[:, None] * jnp.arange(modulus)[None, :] % modulus).astype(jnp.float32)
        / modulus
    )
    return (jnp.cos(angle), jnp.sin(angle))


def finish_transform(twisted_real, twisted_imag):
    highest = lax.Precision.HIGHEST
    cos_table, sin_table = dft_table(SUBLEN, SUBLEN)
    out_real = jnp.einsum("dafs,ac->dcfs", twisted_real, cos_table, precision=highest) + jnp.einsum(
        "dafs,ac->dcfs", twisted_imag, sin_table, precision=highest
    )
    out_imag = jnp.einsum("dafs,ac->dcfs", twisted_imag, cos_table, precision=highest) - jnp.einsum(
        "dafs,ac->dcfs", twisted_real, sin_table, precision=highest
    )
    return jnp.stack([out_real, out_imag]).astype(jnp.bfloat16)


def body(volts, fir, gains, delays, subsets, beam_sizes, station_ids, beam_order):
    highest = lax.Precision.HIGHEST
    taps = fir.shape[0]
    stn_dev = volts.shape[1]
    frames_dev = volts.shape[2] - taps + 1
    filtered = jnp.zeros((2, stn_dev, frames_dev, NCH), jnp.float32)
    for tap_index in range(taps):
        filtered = filtered + fir[tap_index] * volts[
            :, :, tap_index : tap_index + frames_dev, :
        ].astype(jnp.float32)
    real_part = filtered[0].reshape(stn_dev, frames_dev, RADIX, SUBLEN)
    imag_part = filtered[1].reshape(stn_dev, frames_dev, RADIX, SUBLEN)
    first_cos, first_sin = dft_table(RADIX, RADIX)
    section_real = jnp.einsum(
        "sfba,bd->dafs", real_part, first_cos, precision=highest
    ) + jnp.einsum("sfba,bd->dafs", imag_part, first_sin, precision=highest)
    section_imag = jnp.einsum(
        "sfba,bd->dafs", imag_part, first_cos, precision=highest
    ) - jnp.einsum("sfba,bd->dafs", real_part, first_sin, precision=highest)
    twist_angle = (
        full_turn
        * (jnp.arange(RADIX)[:, None] * jnp.arange(SUBLEN)[None, :] % NCH).astype(jnp.float32)
        / NCH
    )
    twist_cos = jnp.cos(twist_angle)[:, :, None, None]
    twist_sin = jnp.sin(twist_angle)[:, :, None, None]
    twisted_real = section_real * twist_cos + section_imag * twist_sin
    twisted_imag = section_imag * twist_cos - section_real * twist_sin
    spectra = finish_transform(twisted_real, twisted_imag).reshape(
        2, RADIX, SUBLEN, frames_dev * stn_dev
    )
    turned = lax.all_to_all(spectra, "chan", split_axis=1, concat_axis=3, tiled=True)
    local_data = lax.all_to_all(turned, "stn", split_axis=2, concat_axis=3, tiled=True)
    radix_local = local_data.shape[1]
    sub_local = local_data.shape[2]
    groups = lax.axis_size("stn")
    frames_all = local_data.shape[3] // (groups * stn_dev)
    grouped = local_data.reshape(2, radix_local, sub_local, groups, frames_all, stn_dev)
    beam_count = subsets.shape[0]
    member = membership(subsets, beam_sizes)
    weight_mask = (
        member[:, station_ids][beam_order]
        * lax.rsqrt(beam_sizes[beam_order].astype(jnp.float32))[:, None]
    )
    delay_rows = delays[:, station_ids][beam_order]
    gain_rows = jnp.take(gains, station_ids, axis=3)
    radix_index = lax.axis_index("chan") * radix_local + jnp.arange(radix_local)
    sub_index = lax.axis_index("stn") * sub_local + jnp.arange(sub_local)
    chan_index = (RADIX * sub_index[None, :] + radix_index[:, None]).astype(jnp.float32)
    angle = (full_turn * chan_index)[:, :, None, None] * delay_rows[None, None] / NCH
    cosine = jnp.cos(angle)
    sine = jnp.sin(angle)
    gain_real = gain_rows[0][:, :, None, :]
    gain_imag = gain_rows[1][:, :, None, :]
    shape_split = (radix_local, sub_local, beam_count, groups, stn_dev)
    weight_real = (
        ((gain_real * cosine + gain_imag * sine) * weight_mask[None, None])
        .astype(jnp.bfloat16)
        .reshape(shape_split)
    )
    weight_imag = (
        ((gain_imag * cosine - gain_real * sine) * weight_mask[None, None])
        .astype(jnp.bfloat16)
        .reshape(shape_split)
    )
    form = "dcbgs,dcgts->dcbt"
    data_real = grouped[0]
    data_imag = grouped[1]
    beam_real = jnp.einsum(
        form, weight_real, data_real, preferred_element_type=jnp.float32
    ) - jnp.einsum(form, weight_imag, data_imag, preferred_element_type=jnp.float32)
    beam_imag = jnp.einsum(
        form, weight_real, data_imag, preferred_element_type=jnp.float32
    ) + jnp.einsum(form, weight_imag, data_real, preferred_element_type=jnp.float32)
    formed = jnp.stack([beam_real, beam_imag]).astype(jnp.bfloat16)
    return lax.all_to_all(formed, "stn", split_axis=3, concat_axis=2, tiled=True)


LANES = 128
ROWS = 8
VMEM_BYTES = 62 * 1024 * 1024


def small_factor(length):
    for factor in (2, 3, 5, 7):
        if length % factor == 0:
            return factor
    return length


def rotate(value, turn):
    real, imag = value
    turn = turn % 1.0
    if turn == 0.0:
        return value
    if turn == 0.5:
        return (-real, -imag)
    if turn == 0.25:
        return (imag, -real)
    if turn == 0.75:
        return (-imag, real)
    cosine, sine = math.cos(full_turn * turn), math.sin(full_turn * turn)
    return (real * cosine + imag * sine, imag * cosine - real * sine)


def short_transform(values):
    length = len(values)
    if length == 1:
        return values
    radix = small_factor(length)
    inner = length // radix
    parts = [short_transform(values[offset::radix]) for offset in range(radix)]
    out = [None] * length
    for low in range(inner):
        terms = [rotate(parts[j][low], j * low / length) for j in range(radix)]
        for high in range(radix):
            total = terms[0]
            for j in range(1, radix):
                turned = rotate(terms[j], j * high / radix)
                total = (total[0] + turned[0], total[1] + turned[1])
            out[low + inner * high] = total
    return out


def swap_granules(tiles, width):
    count = len(tiles)
    lane = lax.broadcasted_iota(jnp.int32, tiles[0].shape, 1)
    bit = 1
    while bit < count:
        shift = bit * width
        low_side = (lane // shift) % 2 == 0
        fresh = list(tiles)
        for index in range(count):
            if index & bit == 0:
                first, second = tiles[index], tiles[index | bit]
                fresh[index] = jnp.where(low_side, first, pltpu.roll(second, shift, 1))
                fresh[index | bit] = jnp.where(
                    low_side, pltpu.roll(first, LANES - shift, 1), second
                )
        tiles = fresh
        bit *= 2
    return tiles


def transform_volts(dims, volts_ref, fir_ref, cos_ref, sin_ref, table_ref, out_ref, kept, rows):
    taps, frames, radix, chan_dev, stn_groups, blocks = dims
    granule = LANES // (2 * frames)

    def filter_tile(b, carry):
        spot = pl.ds(pl.multiple_of(b * LANES, LANES), LANES)
        for part in range(2):
            block = volts_ref[part, :, :, spot].astype(jnp.float32)
            for frame in range(frames):
                total = fir_ref[0:1, spot] * block[frame]
                for tap in range(1, taps):
                    total = total + fir_ref[tap : tap + 1, spot] * block[frame + tap]
                kept[part, frame, b] = total
        return carry

    lax.fori_loop(0, radix, filter_tile, 0)
    pairs = radix // 2
    for frame in range(frames):
        section = short_transform(
            [(kept[0, frame, b], kept[1, frame, b]) for b in range(radix)]
        )
        for d in range(radix):
            real, imag = section[d]
            cosine, sine = cos_ref[d : d + 1, :], sin_ref[d : d + 1, :]
            start = (((d % 2) * frames + frame) * pairs + d // 2) * ROWS
            rows[start : start + ROWS, :LANES] = real * cosine + imag * sine
            rows[start : start + ROWS, LANES:] = imag * cosine - real * sine
    spectra = jnp.dot(
        rows[...],
        table_ref[...],
        preferred_element_type=jnp.float32,
        precision=lax.Precision.HIGHEST,
    )
    size = pairs * ROWS
    share = size // chan_dev
    part = share // blocks
    per_tile = LANES // granule
    for high in range(stn_groups // per_tile):
        tiles = swap_granules(
            [
                spectra[ef * size : (ef + 1) * size, high * LANES : (high + 1) * LANES]
                for ef in range(2 * frames)
            ],
            granule,
        )
        for low in range(per_tile):
            for chan in range(chan_dev):
                for step in range(blocks):
                    start = chan * share + step * part
                    out_ref[step, chan * stn_groups + high * per_tile + low] = tiles[low][
                        start : start + part
                    ].astype(jnp.bfloat16)


def one_hot(ids, size):
    rows = lax.broadcasted_iota(jnp.int32, (size, ids.shape[1]), 0)
    return jnp.where(rows == ids, 1.0, 0.0)


def exact(left, right, transposed=False):
    contract = ((0 if transposed else 1,), (0,))
    return lax.dot_general(
        left,
        right,
        (contract, ((), ())),
        precision=lax.Precision.HIGHEST,
        preferred_element_type=jnp.float32,
    )


def whole_kernel(
    dims,
    volts_in,
    fir_in,
    cos_in,
    sin_in,
    table_in,
    gain_in,
    delay_in,
    subset_in,
    ids_in,
    sizes_in,
    order_in,
    out_ref,
    volts_ref,
    fir_ref,
    cos_ref,
    sin_ref,
    table_ref,
    gain_ref,
    delay_ref,
    subset_ref,
    ids_ref,
    sizes_ref,
    order_ref,
    load_sems,
    kept,
    rows,
    piece_ref,
    data,
    listed,
    member,
    picked,
    delay_rows,
    gain_rows,
    state,
    turns,
    weights,
    rhs,
    formed,
    landed,
    spread,
    in_send,
    in_recv,
    out_send,
    out_recv,
):
    group, subs, chan_dev, stn_groups, frames_all, radix_local = dims
    beams, stations = delay_ref.shape
    radix = radix_local * chan_dev
    channels = fir_ref.shape[1]
    taps = fir_ref.shape[0]
    blocks = radix_local // group
    per_dest = beams // stn_groups
    rows_each = group * per_dest
    devices = chan_dev * stn_groups
    row_block = 2 * ROWS
    my_chan, my_stn = lax.axis_index("chan"), lax.axis_index("stn")
    me = my_chan * stn_groups + my_stn

    def place(peer):
        return {"chan": peer // stn_groups, "stn": peer % stn_groups}

    barrier = pltpu.get_barrier_semaphore()

    def greet(offset, carry):
        peer = (me + offset) % devices
        pl.semaphore_signal(
            barrier, inc=1, device_id=place(peer), device_id_type=pl.DeviceIdType.MESH
        )
        return carry

    loads = [
        pltpu.make_async_copy(source, target, load_sems.at[index])
        for index, (source, target) in enumerate(
            (
                (volts_in, volts_ref),
                (fir_in, fir_ref),
                (cos_in, cos_ref),
                (sin_in, sin_ref),
                (table_in, table_ref),
                (sizes_in, sizes_ref),
                (order_in, order_ref),
                (subset_in, subset_ref),
                (ids_in, ids_ref),
                (delay_in, delay_ref),
                (gain_in, gain_ref),
            )
        )
    ]
    for load in loads:
        load.start()
    lax.fori_loop(1, devices, greet, 0)
    for load in loads:
        load.wait()
    transform_volts(
        (taps, frames_all // chan_dev, radix, chan_dev, stn_groups, blocks),
        volts_ref, fir_ref, cos_ref, sin_ref, table_ref, piece_ref, kept, rows,
    )
    ordered = one_hot(order_ref[...][None, :], beams)
    ordered_narrow = ordered.astype(jnp.bfloat16)
    sizes = jnp.dot(
        jnp.broadcast_to(sizes_ref[...][None, :], (ROWS, beams)).astype(jnp.float32).astype(jnp.bfloat16),
        ordered_narrow,
        preferred_element_type=jnp.float32,
    )[0:1, :]
    entries = lax.dot_general(
        subset_ref[...].astype(jnp.float32).astype(jnp.bfloat16),
        ordered_narrow,
        (((0,), (0,)), ((), ())),
        preferred_element_type=jnp.float32,
    )
    position = lax.broadcasted_iota(jnp.int32, (stations, beams), 0).astype(jnp.float32)
    listed[...] = jnp.where(position < sizes, entries, -1.0)
    scale = lax.rsqrt(sizes)
    block = 4 * ROWS
    for start in range(0, stations, block):
        ids = (lax.broadcasted_iota(jnp.int32, (block, beams), 0) + start).astype(jnp.float32)

        def look(p, total):
            entries = listed[pl.ds(pl.multiple_of(p * ROWS, ROWS), ROWS), :]
            for row in range(ROWS):
                total = jnp.where(entries[row : row + 1, :] == ids, 1.0, total)
            return total

        found = lax.fori_loop(
            0, stations // ROWS, look, jnp.zeros((block, beams), jnp.float32)
        )
        member[start : start + block, :] = found * scale
    station_pick = one_hot(ids_ref[...][None, :], stations)
    picked[...] = exact(member[...], station_pick, transposed=True)
    delay_rows[...] = exact(ordered, exact(delay_ref[...], station_pick), transposed=True)
    gain_rows[...] = exact(gain_ref[...], station_pick)
    first_chan = (radix * subs * my_stn + radix_local * my_chan).astype(jnp.float32)

    def phase(delay, step):
        turn = delay * (step / channels)
        angle = (turn - jnp.round(turn)) * full_turn
        return jnp.cos(angle), jnp.sin(angle)

    def begin(index, carry):
        spot = pl.ds(pl.multiple_of(index * row_block, row_block), row_block)
        delay, mask = delay_rows[spot, :], picked[spot, :]
        cosine, sine = phase(delay, first_chan)
        jump_cos, jump_sin = phase(delay, float(radix))
        turns[0, spot, :], turns[1, spot, :] = phase(delay, 1.0)
        real, imag = cosine * mask, -sine * mask
        for sub in range(subs):
            state[0, sub, spot, :] = real
            state[1, sub, spot, :] = imag
            real, imag = real * jump_cos + imag * jump_sin, imag * jump_cos - real * jump_sin
        return carry

    lax.fori_loop(0, beams // row_block, begin, 0)
    pl.semaphore_wait(barrier, devices - 1)

    def piece_copy(step, peer, slot):
        return pltpu.make_async_remote_copy(
            src_ref=piece_ref.at[step, peer],
            dst_ref=data.at[step, slot],
            send_sem=in_send.at[step, peer],
            recv_sem=in_recv.at[step, slot],
            device_id=place(peer),
            device_id_type=pl.DeviceIdType.MESH,
        )

    def send_pieces(step, carry):
        def send_piece(offset, inner):
            piece_copy(step, (me + offset) % devices, me).start()
            return inner

        lax.fori_loop(1, devices, send_piece, 0)
        data[step, me] = piece_ref[step, me]
        return carry

    lax.fori_loop(0, blocks, send_pieces, 0)

    def weigh(index, carry):
        spot = pl.ds(pl.multiple_of(index * row_block, row_block), row_block)
        cosine, sine = turns[0, spot, :], turns[1, spot, :]
        for sub in range(subs):
            at = 2 * stations * sub
            real, imag = state[0, sub, spot, :], state[1, sub, spot, :]
            for local in range(group):
                weights[local, spot, at : at + stations] = real.astype(jnp.bfloat16)
                weights[local, spot, at + stations : at + 2 * stations] = imag.astype(jnp.bfloat16)
                real, imag = real * cosine + imag * sine, imag * cosine - real * sine
            state[0, sub, spot, :] = real
            state[1, sub, spot, :] = imag
        return carry

    lax.fori_loop(0, beams // row_block, weigh, 0)

    lane = lax.broadcasted_iota(jnp.int32, (stations, LANES), 1)
    is_real = (lane // subs) % 2 == 0
    sub_of = lane % subs
    half = LANES // chan_dev

    def exchange(value):
        return jnp.where(
            is_real, pltpu.roll(value, LANES - subs, 1), pltpu.roll(value, subs, 1)
        )

    def beam_copy(step, stn, slot):
        return pltpu.make_async_remote_copy(
            src_ref=formed.at[step, stn],
            dst_ref=landed.at[step, slot],
            send_sem=out_send.at[step, stn],
            recv_sem=out_recv.at[step, slot],
            device_id={"chan": my_chan, "stn": stn},
            device_id_type=pl.DeviceIdType.MESH,
        )

    def form(step, carry):
        def take_piece(offset, inner):
            peer = (me + offset) % devices
            piece_copy(step, peer, peer).wait_recv()
            return inner

        lax.fori_loop(1, devices, take_piece, 0)
        for local in range(group):
            at = (local // 2) * ROWS
            blocks_in = [
                data[step, c * stn_groups : (c + 1) * stn_groups, at : at + ROWS, :]
                .astype(jnp.float32)
                .reshape(stations, LANES)
                for c in range(2)
            ]
            if local % 2 == 0:
                both = jnp.where(lane < half, blocks_in[0], pltpu.roll(blocks_in[1], half, 1))
            else:
                both = jnp.where(lane < half, pltpu.roll(blocks_in[0], half, 1), blocks_in[1])
            gain_real, gain_imag = (
                jnp.concatenate(
                    [
                        gain_rows[
                            pl.ds(
                                pl.multiple_of(
                                    (part * radix_local + step * group + local) * subs, subs
                                ),
                                subs,
                            ),
                            :,
                        ]
                    ]
                    * (LANES // subs),
                    axis=0,
                ).T
                for part in range(2)
            )
            top = gain_real * both + jnp.where(is_real, -gain_imag, gain_imag) * exchange(both)
            bottom = exchange(top)
            bottom = jnp.where(is_real, -bottom, bottom)
            for sub in range(subs):
                at = 2 * stations * sub
                chosen = sub_of == sub
                rhs[at : at + stations, :] = jnp.where(chosen, top, 0.0).astype(jnp.bfloat16)
                rhs[at + stations : at + 2 * stations, :] = jnp.where(
                    chosen, bottom, 0.0
                ).astype(jnp.bfloat16)
            result = jnp.dot(
                weights[local], rhs[...], preferred_element_type=jnp.float32
            )
            for dest in range(stn_groups):
                formed[step, dest, local * per_dest : (local + 1) * per_dest, :] = result[
                    dest * per_dest : (dest + 1) * per_dest
                ].astype(jnp.bfloat16)

        def send_beams(offset, inner):
            beam_copy(step, (my_stn + offset) % stn_groups, my_stn).start()
            return inner

        lax.fori_loop(1, stn_groups, send_beams, 0)
        landed[step, my_stn] = formed[step, my_stn]

        @pl.when(step < blocks - 1)
        def _():
            lax.fori_loop(0, beams // row_block, weigh, 0)

        return carry

    lax.fori_loop(0, blocks, form, 0)

    def finish(step, carry):
        def take_beams(offset, inner):
            stn = (my_stn + offset) % stn_groups
            beam_copy(step, stn, stn).wait_recv()
            return inner

        lax.fori_loop(1, stn_groups, take_beams, 0)
        tiles = swap_granules(
            [landed[step, source].astype(jnp.float32) for source in range(stn_groups)],
            LANES // stn_groups,
        )
        for part in range(2):
            for t in range(frames_all):
                spread[pl.ds(t, rows_each, stride=frames_all), :] = tiles[2 * t + part]
            out_ref[part, step] = spread[: rows_each * frames_all, :].astype(jnp.bfloat16)
        return carry

    lax.fori_loop(0, blocks, finish, 0)

    def settle_pieces(step, carry):
        def settle(offset, inner):
            piece_copy(step, (me + offset) % devices, me).wait_send()
            return inner

        lax.fori_loop(1, devices, settle, 0)
        return carry

    lax.fori_loop(0, blocks, settle_pieces, 0)

    def settle_beams(step, carry):
        def settle(offset, inner):
            beam_copy(step, (my_stn + offset) % stn_groups, my_stn).wait_send()
            return inner

        lax.fori_loop(1, stn_groups, settle, 0)
        return carry

    lax.fori_loop(0, blocks, settle_beams, 0)


def fused_body(group, volts, fir, gains, delays, subsets, beam_sizes, station_ids, beam_order):
    f32, bf16 = jnp.float32, jnp.bfloat16
    taps = fir.shape[0]
    stn_dev = volts.shape[1]
    frames = volts.shape[2] - taps + 1
    chan_dev = lax.axis_size("chan")
    groups = lax.axis_size("stn")
    radix_local, subs, stations = gains.shape[1:]
    beams = delays.shape[0]
    radix = radix_local * chan_dev
    channels = fir.shape[1]
    sublen = channels // radix
    pairs = radix_local // 2
    per_dest = beams // groups
    frames_all = frames * chan_dev

    turn = np.arange(radix)[:, None] * np.arange(sublen)[None, :] * (2 * np.pi / channels)
    index = np.arange(sublen)
    angle = (index[:, None] * index[None, :] % sublen) * (2 * np.pi / sublen)
    cosine, sine = np.cos(angle), np.sin(angle)
    table = np.stack([np.stack([cosine, -sine], 1), np.stack([sine, cosine], 1)])
    table = table.reshape(2 * sublen, 2, groups, subs).transpose(0, 2, 1, 3)
    table = table.reshape(2 * sublen, 2 * sublen).astype(np.float32)

    blocks = radix_local // group
    rows_each = group * per_dest
    devices = chan_dev * groups
    operands = (
        volts.transpose(0, 2, 1, 3),
        fir,
        jnp.asarray(np.cos(turn), f32),
        jnp.asarray(np.sin(turn), f32),
        jnp.asarray(table),
        gains.reshape(2 * radix_local * subs, stations),
        delays,
        subsets,
        station_ids,
        beam_sizes,
        beam_order,
    )
    done = pl.pallas_call(
        functools.partial(whole_kernel, (group, subs, chan_dev, groups, frames_all, radix_local)),
        in_specs=[pl.BlockSpec(memory_space=pltpu.HBM)] * len(operands),
        out_specs=pl.BlockSpec(memory_space=pltpu.VMEM),
        out_shape=pltpu.VMEM((2, blocks, rows_each * frames_all, LANES), bf16),
        scratch_shapes=[pltpu.VMEM(value.shape, value.dtype) for value in operands]
        + [
            pltpu.SemaphoreType.DMA((len(operands),)),
            pltpu.VMEM((2, frames, radix, stn_dev, LANES), f32),
            pltpu.VMEM((radix * frames * stn_dev, 2 * LANES), f32),
            pltpu.VMEM((blocks, devices, group // 2 * ROWS, LANES), bf16),
            pltpu.VMEM((blocks, devices, group // 2 * ROWS, LANES), bf16),
            pltpu.VMEM((stations, beams), f32),
            pltpu.VMEM((stations, beams), f32),
            pltpu.VMEM((beams, stations), f32),
            pltpu.VMEM((beams, stations), f32),
            pltpu.VMEM((2 * radix_local * subs, stations), f32),
            pltpu.VMEM((2, subs, beams, stations), f32),
            pltpu.VMEM((2, beams, stations), f32),
            pltpu.VMEM((group, beams, 2 * stations * subs), bf16),
            pltpu.VMEM((2 * stations * subs, LANES), bf16),
            pltpu.VMEM((blocks, groups, rows_each, LANES), bf16),
            pltpu.VMEM((blocks, groups, rows_each, LANES), bf16),
            pltpu.VMEM((rows_each * frames_all, LANES), f32),
            pltpu.SemaphoreType.DMA((blocks, devices)),
            pltpu.SemaphoreType.DMA((blocks, devices)),
            pltpu.SemaphoreType.DMA((blocks, groups)),
            pltpu.SemaphoreType.DMA((blocks, groups)),
        ],
        compiler_params=pltpu.CompilerParams(
            collective_id=0, has_side_effects=True, vmem_limit_bytes=VMEM_BYTES
        ),
        name="whole",
    )(*operands)
    done = done.reshape(2, radix_local, per_dest, frames_all, sublen)
    return done.transpose(0, 1, 4, 2, 3)


def group_size(mesh, volts, fir, gains, delays):
    chan_dev, stn_groups = mesh.shape["chan"], mesh.shape["stn"]
    radix_local, subs = gains.shape[1] // chan_dev, gains.shape[2] // stn_groups
    stations, beams = gains.shape[3], delays.shape[0]
    frames = volts.shape[2] // chan_dev - fir.shape[0] + 1
    fits = (
        chan_dev == 2
        and volts.shape[1] // stn_groups == ROWS
        and gains.shape[2] == LANES
        and stations == LANES
        and subs * stn_groups == LANES
        and subs * 2 * frames * chan_dev == LANES
        and stn_groups == 2 * frames * chan_dev
        and beams % (2 * ROWS) == 0
        and radix_local % 2 == 0
    )
    if fits:
        for group in range(2, radix_local + 1, 2):
            if radix_local % group == 0 and group * (beams // stn_groups) % ROWS == 0:
                return group
    return 0


def solution(mesh):
    placed = (
        P(None, "stn", "chan", None),
        P(),
        P(None, "chan", "stn", None),
        P(),
        P(),
        P(),
        P(),
        P(),
    )

    def run(volts, fir, gains, delays, *others):
        group = group_size(mesh, volts, fir, gains, delays)
        return jax.shard_map(
            functools.partial(fused_body, group) if group else body,
            mesh=mesh,
            in_specs=placed,
            out_specs=P(None, "chan", None, "stn", None),
            check_vma=False,
        )(volts, fir, gains, delays, *others)

    return run
```

```python
import functools
import math

import jax
import jax.numpy as jnp
import numpy as np
from jax import lax
from jax.experimental import pallas as pl
from jax.experimental.pallas import tpu as pltpu
from jax.sharding import PartitionSpec as P

RADIX = 24
SUBLEN = 128
NCH = 3072


full_turn = 2.0 * math.pi


def membership(subsets, beam_sizes):
    beam_count = subsets.shape[0]
    station_count = subsets.shape[1]
    block_count = 8
    per_block = beam_count // block_count
    station_range = jnp.arange(station_count, dtype=jnp.int32)

    def one_block(inputs):
        rows, sizes = inputs
        valid = station_range[None, :] < sizes[:, None]
        listed = rows[:, :, None] == station_range[None, None, :]
        return jnp.any(listed & valid[:, :, None], axis=1).astype(jnp.float32)

    blocked = lax.map(
        one_block,
        (
            subsets.reshape(block_count, per_block, station_count),
            beam_sizes.reshape(block_count, per_block),
        ),
    )
    return blocked.reshape(beam_count, station_count)


def dft_table(length, modulus):
    index = jnp.arange(length)
    angle = (
        full_turn
        * (index[:, None] * jnp.arange(modulus)[None, :] % modulus).astype(jnp.float32)
        / modulus
    )
    return (jnp.cos(angle), jnp.sin(angle))


def finish_transform(twisted_real, twisted_imag):
    highest = lax.Precision.HIGHEST
    cos_table, sin_table = dft_table(SUBLEN, SUBLEN)
    out_real = jnp.einsum("dafs,ac->dcfs", twisted_real, cos_table, precision=highest) + jnp.einsum(
        "dafs,ac->dcfs", twisted_imag, sin_table, precision=highest
    )
    out_imag = jnp.einsum("dafs,ac->dcfs", twisted_imag, cos_table, precision=highest) - jnp.einsum(
        "dafs,ac->dcfs", twisted_real, sin_table, precision=highest
    )
    return jnp.stack([out_real, out_imag]).astype(jnp.bfloat16)


def body(volts, fir, gains, delays, subsets, beam_sizes, station_ids, beam_order):
    highest = lax.Precision.HIGHEST
    taps = fir.shape[0]
    stn_dev = volts.shape[1]
    frames_dev = volts.shape[2] - taps + 1
    filtered = jnp.zeros((2, stn_dev, frames_dev, NCH), jnp.float32)
    for tap_index in range(taps):
        filtered = filtered + fir[tap_index] * volts[
            :, :, tap_index : tap_index + frames_dev, :
        ].astype(jnp.float32)
    real_part = filtered[0].reshape(stn_dev, frames_dev, RADIX, SUBLEN)
    imag_part = filtered[1].reshape(stn_dev, frames_dev, RADIX, SUBLEN)
    first_cos, first_sin = dft_table(RADIX, RADIX)
    section_real = jnp.einsum(
        "sfba,bd->dafs", real_part, first_cos, precision=highest
    ) + jnp.einsum("sfba,bd->dafs", imag_part, first_sin, precision=highest)
    section_imag = jnp.einsum(
        "sfba,bd->dafs", imag_part, first_cos, precision=highest
    ) - jnp.einsum("sfba,bd->dafs", real_part, first_sin, precision=highest)
    twist_angle = (
        full_turn
        * (jnp.arange(RADIX)[:, None] * jnp.arange(SUBLEN)[None, :] % NCH).astype(jnp.float32)
        / NCH
    )
    twist_cos = jnp.cos(twist_angle)[:, :, None, None]
    twist_sin = jnp.sin(twist_angle)[:, :, None, None]
    twisted_real = section_real * twist_cos + section_imag * twist_sin
    twisted_imag = section_imag * twist_cos - section_real * twist_sin
    spectra = finish_transform(twisted_real, twisted_imag).reshape(
        2, RADIX, SUBLEN, frames_dev * stn_dev
    )
    turned = lax.all_to_all(spectra, "chan", split_axis=1, concat_axis=3, tiled=True)
    local_data = lax.all_to_all(turned, "stn", split_axis=2, concat_axis=3, tiled=True)
    radix_local = local_data.shape[1]
    sub_local = local_data.shape[2]
    groups = lax.axis_size("stn")
    frames_all = local_data.shape[3] // (groups * stn_dev)
    grouped = local_data.reshape(2, radix_local, sub_local, groups, frames_all, stn_dev)
    beam_count = subsets.shape[0]
    member = membership(subsets, beam_sizes)
    weight_mask = (
        member[:, station_ids][beam_order]
        * lax.rsqrt(beam_sizes[beam_order].astype(jnp.float32))[:, None]
    )
    delay_rows = delays[:, station_ids][beam_order]
    gain_rows = jnp.take(gains, station_ids, axis=3)
    radix_index = lax.axis_index("chan") * radix_local + jnp.arange(radix_local)
    sub_index = lax.axis_index("stn") * sub_local + jnp.arange(sub_local)
    chan_index = (RADIX * sub_index[None, :] + radix_index[:, None]).astype(jnp.float32)
    angle = (full_turn * chan_index)[:, :, None, None] * delay_rows[None, None] / NCH
    cosine = jnp.cos(angle)
    sine = jnp.sin(angle)
    gain_real = gain_rows[0][:, :, None, :]
    gain_imag = gain_rows[1][:, :, None, :]
    shape_split = (radix_local, sub_local, beam_count, groups, stn_dev)
    weight_real = (
        ((gain_real * cosine + gain_imag * sine) * weight_mask[None, None])
        .astype(jnp.bfloat16)
        .reshape(shape_split)
    )
    weight_imag = (
        ((gain_imag * cosine - gain_real * sine) * weight_mask[None, None])
        .astype(jnp.bfloat16)
        .reshape(shape_split)
    )
    form = "dcbgs,dcgts->dcbt"
    data_real = grouped[0]
    data_imag = grouped[1]
    beam_real = jnp.einsum(
        form, weight_real, data_real, preferred_element_type=jnp.float32
    ) - jnp.einsum(form, weight_imag, data_imag, preferred_element_type=jnp.float32)
    beam_imag = jnp.einsum(
        form, weight_real, data_imag, preferred_element_type=jnp.float32
    ) + jnp.einsum(form, weight_imag, data_real, preferred_element_type=jnp.float32)
    formed = jnp.stack([beam_real, beam_imag]).astype(jnp.bfloat16)
    return lax.all_to_all(formed, "stn", split_axis=3, concat_axis=2, tiled=True)


LANES = 128
ROWS = 8
VMEM_BYTES = 62 * 1024 * 1024


def small_factor(length):
    for factor in (2, 3, 5, 7):
        if length % factor == 0:
            return factor
    return length


def rotate(value, turn):
    real, imag = value
    turn = turn % 1.0
    if turn == 0.0:
        return value
    if turn == 0.5:
        return (-real, -imag)
    if turn == 0.25:
        return (imag, -real)
    if turn == 0.75:
        return (-imag, real)
    cosine, sine = math.cos(full_turn * turn), math.sin(full_turn * turn)
    return (real * cosine + imag * sine, imag * cosine - real * sine)


def short_transform(values):
    length = len(values)
    if length == 1:
        return values
    radix = small_factor(length)
    inner = length // radix
    parts = [short_transform(values[offset::radix]) for offset in range(radix)]
    out = [None] * length
    for low in range(inner):
        terms = [rotate(parts[j][low], j * low / length) for j in range(radix)]
        for high in range(radix):
            total = terms[0]
            for j in range(1, radix):
                turned = rotate(terms[j], j * high / radix)
                total = (total[0] + turned[0], total[1] + turned[1])
            out[low + inner * high] = total
    return out


def swap_granules(tiles, width):
    count = len(tiles)
    lane = lax.broadcasted_iota(jnp.int32, tiles[0].shape, 1)
    bit = 1
    while bit < count:
        shift = bit * width
        low_side = (lane // shift) % 2 == 0
        fresh = list(tiles)
        for index in range(count):
            if index & bit == 0:
                first, second = tiles[index], tiles[index | bit]
                fresh[index] = jnp.where(low_side, first, pltpu.roll(second, shift, 1))
                fresh[index | bit] = jnp.where(
                    low_side, pltpu.roll(first, LANES - shift, 1), second
                )
        tiles = fresh
        bit *= 2
    return tiles


def transform_volts(dims, volts_ref, fir_ref, cos_ref, sin_ref, table_ref, out_ref, kept, rows):
    taps, frames, radix, chan_dev, stn_groups, blocks = dims
    granule = LANES // (2 * frames)

    def filter_tile(b, carry):
        spot = pl.ds(pl.multiple_of(b * LANES, LANES), LANES)
        for part in range(2):
            block = volts_ref[part, :, :, spot].astype(jnp.float32)
            for frame in range(frames):
                total = fir_ref[0:1, spot] * block[frame]
                for tap in range(1, taps):
                    total = total + fir_ref[tap : tap + 1, spot] * block[frame + tap]
                kept[part, frame, b] = total
        return carry

    lax.fori_loop(0, radix, filter_tile, 0)
    pairs = radix // 2
    for frame in range(frames):
        section = short_transform(
            [(kept[0, frame, b], kept[1, frame, b]) for b in range(radix)]
        )
        for d in range(radix):
            real, imag = section[d]
            cosine, sine = cos_ref[d : d + 1, :], sin_ref[d : d + 1, :]
            start = (((d % 2) * frames + frame) * pairs + d // 2) * ROWS
            rows[start : start + ROWS, :LANES] = real * cosine + imag * sine
            rows[start : start + ROWS, LANES:] = imag * cosine - real * sine
    spectra = jnp.dot(
        rows[...],
        table_ref[...],
        preferred_element_type=jnp.float32,
        precision=lax.Precision.HIGHEST,
    )
    size = pairs * ROWS
    share = size // chan_dev
    part = share // blocks
    per_tile = LANES // granule
    for high in range(stn_groups // per_tile):
        tiles = swap_granules(
            [
                spectra[ef * size : (ef + 1) * size, high * LANES : (high + 1) * LANES]
                for ef in range(2 * frames)
            ],
            granule,
        )
        for low in range(per_tile):
            for chan in range(chan_dev):
                for step in range(blocks):
                    start = chan * share + step * part
                    out_ref[step, chan * stn_groups + high * per_tile + low] = tiles[low][
                        start : start + part
                    ].astype(jnp.bfloat16)


def one_hot(ids, size):
    rows = lax.broadcasted_iota(jnp.int32, (size, ids.shape[1]), 0)
    return jnp.where(rows == ids, 1.0, 0.0).astype(jnp.bfloat16)


def split(value):
    parts = []
    for _ in range(2):
        part = value.astype(jnp.bfloat16)
        parts.append(part)
        value = value - part.astype(jnp.float32)
    return parts + [value.astype(jnp.bfloat16)]


def pick(value, chosen, left=0):
    return lax.dot_general(
        jnp.concatenate(split(value), axis=left),
        jnp.concatenate([chosen] * 3, axis=0),
        (((left,), (0,)), ((), ())),
        preferred_element_type=jnp.float32,
    )


def whole_kernel(
    dims,
    volts_in,
    fir_in,
    cos_in,
    sin_in,
    table_in,
    gain_in,
    delay_in,
    subset_in,
    ids_in,
    sizes_in,
    order_in,
    out_ref,
    volts_ref,
    fir_ref,
    cos_ref,
    sin_ref,
    table_ref,
    gain_ref,
    delay_ref,
    subset_ref,
    ids_ref,
    sizes_ref,
    order_ref,
    load_sems,
    kept,
    rows,
    piece_ref,
    data,
    listed,
    member,
    picked,
    delay_rows,
    gain_rows,
    state,
    turns,
    weights,
    rhs,
    formed,
    landed,
    spread,
    in_send,
    in_recv,
    out_send,
    out_recv,
):
    group, subs, chan_dev, stn_groups, frames_all, radix_local = dims
    beams, stations = delay_ref.shape
    radix = radix_local * chan_dev
    channels = fir_ref.shape[1]
    taps = fir_ref.shape[0]
    blocks = radix_local // group
    per_dest = beams // stn_groups
    rows_each = group * per_dest
    devices = chan_dev * stn_groups
    row_block = 2 * ROWS
    my_chan, my_stn = lax.axis_index("chan"), lax.axis_index("stn")
    me = my_chan * stn_groups + my_stn

    def place(peer):
        return {"chan": peer // stn_groups, "stn": peer % stn_groups}

    barrier = pltpu.get_barrier_semaphore()

    def greet(offset, carry):
        peer = (me + offset) % devices
        pl.semaphore_signal(
            barrier, inc=1, device_id=place(peer), device_id_type=pl.DeviceIdType.MESH
        )
        return carry

    loads = [
        pltpu.make_async_copy(source, target, load_sems.at[index])
        for index, (source, target) in enumerate(
            (
                (volts_in, volts_ref),
                (fir_in, fir_ref),
                (cos_in, cos_ref),
                (sin_in, sin_ref),
                (table_in, table_ref),
                (sizes_in, sizes_ref),
                (order_in, order_ref),
                (subset_in, subset_ref),
                (ids_in, ids_ref),
                (delay_in, delay_ref),
                (gain_in, gain_ref),
            )
        )
    ]
    for load in loads:
        load.start()
    lax.fori_loop(1, devices, greet, 0)
    for load in loads:
        load.wait()
    transform_volts(
        (taps, frames_all // chan_dev, radix, chan_dev, stn_groups, blocks),
        volts_ref, fir_ref, cos_ref, sin_ref, table_ref, piece_ref, kept, rows,
    )
    ordered = one_hot(order_ref[...][None, :], beams)
    sizes = jnp.dot(
        jnp.broadcast_to(sizes_ref[...][None, :], (ROWS, beams)).astype(jnp.float32).astype(jnp.bfloat16),
        ordered,
        preferred_element_type=jnp.float32,
    )[0:1, :]
    entries = lax.dot_general(
        subset_ref[...].astype(jnp.float32).astype(jnp.bfloat16),
        ordered,
        (((0,), (0,)), ((), ())),
        preferred_element_type=jnp.float32,
    )
    position = lax.broadcasted_iota(jnp.int32, (stations, beams), 0).astype(jnp.float32)
    listed[...] = jnp.where(position < sizes, entries, -1.0)
    scale = lax.rsqrt(sizes)
    block = 4 * ROWS
    for start in range(0, stations, block):
        ids = (lax.broadcasted_iota(jnp.int32, (block, beams), 0) + start).astype(jnp.float32)

        def look(p, total):
            entries = listed[pl.ds(pl.multiple_of(p * ROWS, ROWS), ROWS), :]
            for row in range(ROWS):
                total = jnp.where(entries[row : row + 1, :] == ids, 1.0, total)
            return total

        found = lax.fori_loop(
            0, stations // ROWS, look, jnp.zeros((block, beams), jnp.float32)
        )
        member[start : start + block, :] = found * scale
    station_pick = one_hot(ids_ref[...][None, :], stations)
    picked[...] = pick(member[...], station_pick)
    delay_rows[...] = pick(pick(delay_ref[...], ordered), station_pick)
    gain_rows[...] = pick(gain_ref[...], station_pick, left=1)
    pl.semaphore_wait(barrier, devices - 1)

    def piece_copy(step, peer, slot):
        return pltpu.make_async_remote_copy(
            src_ref=piece_ref.at[step, peer],
            dst_ref=data.at[step, slot],
            send_sem=in_send.at[step, peer],
            recv_sem=in_recv.at[step, slot],
            device_id=place(peer),
            device_id_type=pl.DeviceIdType.MESH,
        )

    def send_pieces(step, carry):
        def send_piece(offset, inner):
            piece_copy(step, (me + offset) % devices, me).start()
            return inner

        lax.fori_loop(1, devices, send_piece, 0)
        data[step, me] = piece_ref[step, me]
        return carry

    lax.fori_loop(0, blocks, send_pieces, 0)

    first_chan = (radix * subs * my_stn + radix_local * my_chan).astype(jnp.float32)

    def phase(delay, step):
        turn = delay * (step / channels)
        angle = (turn - jnp.round(turn)) * full_turn
        return jnp.cos(angle), jnp.sin(angle)

    def begin(index, carry):
        spot = pl.ds(pl.multiple_of(index * row_block, row_block), row_block)
        delay, mask = delay_rows[spot, :], picked[spot, :]
        cosine, sine = phase(delay, first_chan)
        jump_cos, jump_sin = phase(delay, float(radix))
        turns[0, spot, :], turns[1, spot, :] = phase(delay, 1.0)
        real, imag = cosine * mask, -sine * mask
        for sub in range(subs):
            state[0, sub, spot, :] = real
            state[1, sub, spot, :] = imag
            real, imag = real * jump_cos + imag * jump_sin, imag * jump_cos - real * jump_sin
        return carry

    lax.fori_loop(0, beams // row_block, begin, 0)

    def weigh(index, carry):
        spot = pl.ds(pl.multiple_of(index * row_block, row_block), row_block)
        cosine, sine = turns[0, spot, :], turns[1, spot, :]
        for sub in range(subs):
            at = 2 * stations * sub
            real, imag = state[0, sub, spot, :], state[1, sub, spot, :]
            for local in range(group):
                weights[local, spot, at : at + stations] = real.astype(jnp.bfloat16)
                weights[local, spot, at + stations : at + 2 * stations] = imag.astype(jnp.bfloat16)
                real, imag = real * cosine + imag * sine, imag * cosine - real * sine
            state[0, sub, spot, :] = real
            state[1, sub, spot, :] = imag
        return carry

    lax.fori_loop(0, beams // row_block, weigh, 0)

    lane = lax.broadcasted_iota(jnp.int32, (stations, LANES), 1)
    is_real = (lane // subs) % 2 == 0
    sub_of = lane % subs
    half = LANES // chan_dev

    def exchange(value):
        return jnp.where(
            is_real, pltpu.roll(value, LANES - subs, 1), pltpu.roll(value, subs, 1)
        )

    def beam_copy(step, stn, slot):
        return pltpu.make_async_remote_copy(
            src_ref=formed.at[step, stn],
            dst_ref=landed.at[step, slot],
            send_sem=out_send.at[step, stn],
            recv_sem=out_recv.at[step, slot],
            device_id={"chan": my_chan, "stn": stn},
            device_id_type=pl.DeviceIdType.MESH,
        )

    def form(step, carry):
        def take_piece(offset, inner):
            peer = (me + offset) % devices
            piece_copy(step, peer, peer).wait_recv()
            return inner

        lax.fori_loop(1, devices, take_piece, 0)
        for local in range(group):
            at = (local // 2) * ROWS
            blocks_in = [
                data[step, c * stn_groups : (c + 1) * stn_groups, at : at + ROWS, :]
                .astype(jnp.float32)
                .reshape(stations, LANES)
                for c in range(2)
            ]
            if local % 2 == 0:
                both = jnp.where(lane < half, blocks_in[0], pltpu.roll(blocks_in[1], half, 1))
            else:
                both = jnp.where(lane < half, pltpu.roll(blocks_in[0], half, 1), blocks_in[1])
            gain_real, gain_imag = (
                jnp.concatenate(
                    [
                        gain_rows[
                            pl.ds(
                                pl.multiple_of(
                                    (part * radix_local + step * group + local) * subs, subs
                                ),
                                subs,
                            ),
                            :,
                        ]
                    ]
                    * (LANES // subs),
                    axis=0,
                ).T
                for part in range(2)
            )
            top = gain_real * both + jnp.where(is_real, -gain_imag, gain_imag) * exchange(both)
            bottom = exchange(top)
            bottom = jnp.where(is_real, -bottom, bottom)
            for sub in range(subs):
                at = 2 * stations * sub
                chosen = sub_of == sub
                rhs[at : at + stations, :] = jnp.where(chosen, top, 0.0).astype(jnp.bfloat16)
                rhs[at + stations : at + 2 * stations, :] = jnp.where(
                    chosen, bottom, 0.0
                ).astype(jnp.bfloat16)
            result = jnp.dot(
                weights[local], rhs[...], preferred_element_type=jnp.float32
            )
            for dest in range(stn_groups):
                formed[step, dest, local * per_dest : (local + 1) * per_dest, :] = result[
                    dest * per_dest : (dest + 1) * per_dest
                ].astype(jnp.bfloat16)

        def send_beams(offset, inner):
            beam_copy(step, (my_stn + offset) % stn_groups, my_stn).start()
            return inner

        lax.fori_loop(1, stn_groups, send_beams, 0)
        landed[step, my_stn] = formed[step, my_stn]

        @pl.when(step < blocks - 1)
        def _():
            lax.fori_loop(0, beams // row_block, weigh, 0)

        return carry

    lax.fori_loop(0, blocks, form, 0)

    def settle_pieces(step, carry):
        def settle(offset, inner):
            piece_copy(step, (me + offset) % devices, me).wait_send()
            return inner

        lax.fori_loop(1, devices, settle, 0)
        return carry

    lax.fori_loop(0, blocks, settle_pieces, 0)

    def settle_beams(step, carry):
        def settle(offset, inner):
            beam_copy(step, (my_stn + offset) % stn_groups, my_stn).wait_send()
            return inner

        lax.fori_loop(1, stn_groups, settle, 0)
        return carry

    lax.fori_loop(0, blocks, settle_beams, 0)

    def finish(step, carry):
        def take_beams(offset, inner):
            stn = (my_stn + offset) % stn_groups
            beam_copy(step, stn, stn).wait_recv()
            return inner

        lax.fori_loop(1, stn_groups, take_beams, 0)
        tiles = swap_granules(
            [landed[step, source].astype(jnp.float32) for source in range(stn_groups)],
            LANES // stn_groups,
        )
        for part in range(2):
            for t in range(frames_all):
                spread[pl.ds(t, rows_each, stride=frames_all), :] = tiles[2 * t + part]
            out_ref[part, step] = spread[: rows_each * frames_all, :].astype(jnp.bfloat16)
        return carry

    lax.fori_loop(0, blocks, finish, 0)


def fused_body(group, volts, fir, gains, delays, subsets, beam_sizes, station_ids, beam_order):
    f32, bf16 = jnp.float32, jnp.bfloat16
    taps = fir.shape[0]
    stn_dev = volts.shape[1]
    frames = volts.shape[2] - taps + 1
    chan_dev = lax.axis_size("chan")
    groups = lax.axis_size("stn")
    radix_local, subs, stations = gains.shape[1:]
    beams = delays.shape[0]
    radix = radix_local * chan_dev
    channels = fir.shape[1]
    sublen = channels // radix
    pairs = radix_local // 2
    per_dest = beams // groups
    frames_all = frames * chan_dev

    turn = np.arange(radix)[:, None] * np.arange(sublen)[None, :] * (2 * np.pi / channels)
    index = np.arange(sublen)
    angle = (index[:, None] * index[None, :] % sublen) * (2 * np.pi / sublen)
    cosine, sine = np.cos(angle), np.sin(angle)
    table = np.stack([np.stack([cosine, -sine], 1), np.stack([sine, cosine], 1)])
    table = table.reshape(2 * sublen, 2, groups, subs).transpose(0, 2, 1, 3)
    table = table.reshape(2 * sublen, 2 * sublen).astype(np.float32)

    blocks = radix_local // group
    rows_each = group * per_dest
    devices = chan_dev * groups
    operands = (
        volts.transpose(0, 2, 1, 3),
        fir,
        jnp.asarray(np.cos(turn), f32),
        jnp.asarray(np.sin(turn), f32),
        jnp.asarray(table),
        gains.reshape(2 * radix_local * subs, stations),
        delays,
        subsets,
        station_ids,
        beam_sizes,
        beam_order,
    )
    done = pl.pallas_call(
        functools.partial(whole_kernel, (group, subs, chan_dev, groups, frames_all, radix_local)),
        in_specs=[pl.BlockSpec(memory_space=pltpu.HBM)] * len(operands),
        out_specs=pl.BlockSpec(memory_space=pltpu.VMEM),
        out_shape=pltpu.VMEM((2, blocks, rows_each * frames_all, LANES), bf16),
        scratch_shapes=[pltpu.VMEM(value.shape, value.dtype) for value in operands]
        + [
            pltpu.SemaphoreType.DMA((len(operands),)),
            pltpu.VMEM((2, frames, radix, stn_dev, LANES), f32),
            pltpu.VMEM((radix * frames * stn_dev, 2 * LANES), f32),
            pltpu.VMEM((blocks, devices, group // 2 * ROWS, LANES), bf16),
            pltpu.VMEM((blocks, devices, group // 2 * ROWS, LANES), bf16),
            pltpu.VMEM((stations, beams), f32),
            pltpu.VMEM((stations, beams), f32),
            pltpu.VMEM((beams, stations), f32),
            pltpu.VMEM((beams, stations), f32),
            pltpu.VMEM((2 * radix_local * subs, stations), f32),
            pltpu.VMEM((2, subs, beams, stations), f32),
            pltpu.VMEM((2, beams, stations), f32),
            pltpu.VMEM((group, beams, 2 * stations * subs), bf16),
            pltpu.VMEM((2 * stations * subs, LANES), bf16),
            pltpu.VMEM((blocks, groups, rows_each, LANES), bf16),
            pltpu.VMEM((blocks, groups, rows_each, LANES), bf16),
            pltpu.VMEM((rows_each * frames_all, LANES), f32),
            pltpu.SemaphoreType.DMA((blocks, devices)),
            pltpu.SemaphoreType.DMA((blocks, devices)),
            pltpu.SemaphoreType.DMA((blocks, groups)),
            pltpu.SemaphoreType.DMA((blocks, groups)),
        ],
        compiler_params=pltpu.CompilerParams(
            collective_id=0, has_side_effects=True, vmem_limit_bytes=VMEM_BYTES
        ),
        name="whole",
    )(*operands)
    done = done.reshape(2, radix_local, per_dest, frames_all, sublen)
    return done.transpose(0, 1, 4, 2, 3)


def group_size(mesh, volts, fir, gains, delays):
    chan_dev, stn_groups = mesh.shape["chan"], mesh.shape["stn"]
    radix_local, subs = gains.shape[1] // chan_dev, gains.shape[2] // stn_groups
    stations, beams = gains.shape[3], delays.shape[0]
    frames = volts.shape[2] // chan_dev - fir.shape[0] + 1
    fits = (
        chan_dev == 2
        and volts.shape[1] // stn_groups == ROWS
        and gains.shape[2] == LANES
        and stations == LANES
        and subs * stn_groups == LANES
        and subs * 2 * frames * chan_dev == LANES
        and stn_groups == 2 * frames * chan_dev
        and beams % (2 * ROWS) == 0
        and radix_local % 2 == 0
    )
    if fits:
        for group in range(2, radix_local + 1, 2):
            if radix_local % group == 0 and group * (beams // stn_groups) % ROWS == 0:
                return group
    return 0


def solution(mesh):
    placed = (
        P(None, "stn", "chan", None),
        P(),
        P(None, "chan", "stn", None),
        P(),
        P(),
        P(),
        P(),
        P(),
    )

    def run(volts, fir, gains, delays, *others):
        group = group_size(mesh, volts, fir, gains, delays)
        return jax.shard_map(
            functools.partial(fused_body, group) if group else body,
            mesh=mesh,
            in_specs=placed,
            out_specs=P(None, "chan", None, "stn", None),
            check_vma=False,
        )(volts, fir, gains, delays, *others)

    return run
```
